512 devices in a mesh: rx: 64 (over z_lo, x, core), band: 8 (over y, z_hi).
Axes of the slice: x: 4, y: 4, z: 16 (z_hi: 2, z_lo: 8; z = z_hi * 8 + z_lo), core: 2. Of those that a mesh axis runs over, the one named last changes fastest.
Arguments:
- spectra: bfloat16 [2, 256, 64, 8192], P(None, 'band', None, 'rx'), may hold values from -6 to 6
- source_index: int32 [64], replicated, may hold values from 0 to 8191, as said below
Outputs:
- stack: bfloat16 [2, 256, 64, 8192], P(None, 'band', None, 'rx')
The draws below stay inside these ranges and needn't reach their ends.
Inputs may be any that keep to these rules, and one draw needn't show every extreme that they name: `source_index`: virtual source s is one of channels s * 128 to (s + 1) * 128 - 1; the first and the last channel are sources.
All inputs are finite; a program needn't handle non-finite values.
Results may differ from the reference program's by a relative error of at most 0.0059.
Values may be sent and summed in bfloat16 or wider, within the bound.
A program may use at most 64 MiB of HBM per device.

```python
import jax
import jax.numpy as jnp
from jax import lax

CH_DEV = 128
WINDOWS = 64
FREQS = 256
HALF = 4
SOURCES = 64
CHANNELS = 8192


def draw_source_index(key, part):
    offsets = jax.random.randint(key, (SOURCES,), 0, CH_DEV, dtype=jnp.int32)
    positions = jnp.arange(SOURCES, dtype=jnp.int32)
    offsets = jnp.where(positions == 0, 0, offsets)
    offsets = jnp.where(positions == SOURCES - 1, CH_DEV - 1, offsets)
    return (positions * CH_DEV + offsets).astype(jnp.int32)


def levels(own_key, extent, pieces, least, largest):
    factor_of = 1.0
    for dim, shards_of in pieces:
        heights = jax.random.uniform(jax.random.fold_in(jax.random.fold_in(own_key, 6), dim), (shards_of,), jnp.float32, least / len(pieces), largest / len(pieces))
        factor_of = factor_of * jnp.repeat(jnp.exp(heights), extent[dim] // shards_of).reshape((-1,) + (1,) * (len(extent) - 1 - dim))
    return factor_of


def scatter_about(own_key, dims, spread, reach, shards=(), kind=jnp.bfloat16):
    entries = jax.random.normal(own_key, dims, jnp.float32) * spread
    if len(shards) > 0:
        entries = levels(own_key, dims, shards, -0.22, 0.18) * entries
    return jnp.clip(entries, min=-reach, max=reach).astype(kind)


def setup_inputs(seed: int = 0) -> dict:
    seeds = jax.random.split(jax.random.key(seed), 3)
    return {
        "spectra": scatter_about(seeds[0], (2, FREQS, WINDOWS, CHANNELS), 1.0, 6.0, ((1, 8), (3, 64))),
        "source_index": draw_source_index(jax.random.fold_in(seeds[2], 71), 0),
    }


def reference(spectra, source_index):
    values = spectra.astype(jnp.float32)
    rounded = lax.optimization_barrier(jnp.sqrt(values[0] * values[0] + values[1] * values[1]).astype(jnp.bfloat16))
    amplitude = rounded.astype(jnp.float32)
    padded_amplitude = jnp.pad(amplitude, ((HALF, HALF), (0, 0), (0, 0)))

    def per_bin(bin_index):
        total = jnp.zeros(amplitude.shape[1:], jnp.float32)
        for offset in range(2 * HALF + 1):
            total = total + lax.dynamic_index_in_dim(padded_amplitude, bin_index + offset, 0, keepdims=False)
        smooth = total / (2 * HALF + 1)
        spectrum_bin = lax.dynamic_index_in_dim(spectra, bin_index, 1, keepdims=False).astype(jnp.float32)
        whitened = (spectrum_bin / (smooth + 0.1)[None]).astype(jnp.bfloat16)
        source_spectra = jnp.take(whitened, source_index, axis=2)
        white_real = whitened[0].astype(jnp.float32)
        white_imag = whitened[1].astype(jnp.float32)
        source_real = source_spectra[0].astype(jnp.float32)
        source_imag = source_spectra[1].astype(jnp.float32)
        real_part = jnp.einsum('wc,ws->sc', white_real, source_real) + jnp.einsum('wc,ws->sc', white_imag, source_imag)
        imag_part = jnp.einsum('wc,ws->sc', white_imag, source_real) - jnp.einsum('wc,ws->sc', white_real, source_imag)
        return (jnp.stack([real_part, imag_part], 0) / WINDOWS).astype(jnp.bfloat16)
    stacked = lax.map(per_bin, jnp.arange(FREQS, dtype=jnp.int32))
    return jnp.transpose(stacked, (1, 0, 2, 3))
```

```python
import functools

import jax
import jax.numpy as jnp
from jax import lax
from jax.experimental import pallas as pl
from jax.experimental.pallas import tpu as pltpu
from jax.sharding import PartitionSpec as P

HALF = 4
BINS = 32
WIN = 64
CH = 128
ROWS = 8
COLS = 8
BANDS = 8
MESH = pl.DeviceIdType.MESH


def gather_kernel(src_ref, x_ref, g_ref, rows, edge_out, edge_in,
                  zs, zr, es, er, js, jr):
    rx = lax.axis_index("rx")
    band = lax.axis_index("band")
    z = lax.div(rx, COLS)
    j = lax.rem(rx, COLS)
    above = lax.rem(band + 1, BANDS)
    below = lax.rem(band + BANDS - 1, BANDS)

    def along_z(d):
        return lax.rem(z + d, ROWS)

    def along_j(d):
        return lax.rem(j + d, COLS)

    barrier = pltpu.get_barrier_semaphore()
    for d in range(1, ROWS):
        pl.semaphore_signal(barrier, inc=1, device_id=(along_z(d) * COLS + j, band), device_id_type=MESH)
    for d in range(1, COLS):
        pl.semaphore_signal(barrier, inc=1, device_id=(z * COLS + along_j(d), band), device_id_type=MESH)
    for d in range(ROWS):
        for other in (above, below):
            pl.semaphore_signal(barrier, inc=1, device_id=(along_z(d) * COLS + j, other), device_id_type=MESH)

    column = src_ref[rx] - rx * CH
    lane = lax.broadcasted_iota(jnp.int32, (BINS, CH), 1)
    bin_row = lax.broadcasted_iota(jnp.int32, (BINS, CH), 0)
    pick = jnp.where(lane == column, 1.0, 0.0).astype(jnp.float32)
    row = jnp.zeros((BINS, CH), jnp.float32)
    for f in range(BINS):
        one = jnp.where(bin_row == f, pick, 0.0).astype(jnp.bfloat16)
        both = x_ref[:, f].reshape(2 * WIN, CH)
        row = row + lax.dot_general(one, both, (((1,), (1,)), ((), ())),
                                    preferred_element_type=jnp.float32)

    def amplitude(values):
        square = values * values
        return jnp.sqrt(square + pltpu.roll(square, WIN, 1)).astype(jnp.bfloat16).astype(jnp.float32)

    own_amp = amplitude(row)
    edge_out[0] = own_amp[0:HALF]
    edge_out[1] = own_amp[BINS - HALF:BINS]
    rows[z] = row.astype(jnp.bfloat16)

    pl.semaphore_wait(barrier, (ROWS - 1) + (COLS - 1) + 2 * ROWS)

    def edge_copy(side, d, slot):
        other = below if side == 0 else above
        return pltpu.make_async_remote_copy(
            src_ref=edge_out.at[side], dst_ref=edge_in.at[1 - side, slot],
            send_sem=es.at[side, d], recv_sem=er.at[side, d],
            device_id=(along_z(d) * COLS + j, other), device_id_type=MESH)

    def row_copy(d, slot):
        return pltpu.make_async_remote_copy(
            src_ref=rows.at[z], dst_ref=rows.at[slot],
            send_sem=zs.at[d], recv_sem=zr.at[d],
            device_id=(along_z(d) * COLS + j, band), device_id_type=MESH)

    for d in (4, 3, 5, 2, 6, 1, 7, 0):
        for side in range(2):
            edge_copy(side, d, z).start()
    for d in (7, 6, 5, 4, 3, 2, 1):
        row_copy(d, z).start()
    for d in range(1, ROWS):
        row_copy(d, lax.rem(z - d + ROWS, ROWS)).wait_recv()
    for d in range(ROWS):
        for side in range(2):
            edge_copy(side, d, lax.rem(z - d + ROWS, ROWS)).wait_recv()

    has_low = (band > 0).astype(jnp.float32)
    has_high = (band < BANDS - 1).astype(jnp.float32)
    for k in range(ROWS):
        values = rows[k].astype(jnp.float32)
        padded = jnp.concatenate(
            [edge_in[0, k] * has_low, amplitude(values), edge_in[1, k] * has_high], axis=0)
        total = padded[0:BINS]
        for offset in range(1, 2 * HALF + 1):
            total = total + padded[offset:offset + BINS]
        smooth = total / (2 * HALF + 1)
        g_ref[j, k] = (values / (smooth + 0.1)).astype(jnp.bfloat16)

    def block_copy(d, slot):
        return pltpu.make_async_remote_copy(
            src_ref=g_ref.at[j], dst_ref=g_ref.at[slot],
            send_sem=js.at[d], recv_sem=jr.at[d],
            device_id=(z * COLS + along_j(d), band), device_id_type=MESH)

    for d in (4, 3, 5, 2, 6, 1, 7):
        block_copy(d, j).start()
    for d in range(1, ROWS):
        row_copy(d, z).wait_send()
    for d in range(ROWS):
        for side in range(2):
            edge_copy(side, d, z).wait_send()
    for d in range(1, COLS):
        block_copy(d, lax.rem(j - d + COLS, COLS)).wait_recv()
    for d in range(1, COLS):
        block_copy(d, j).wait_send()


def stack_kernel(x_ref, low_ref, high_ref, g_ref, out_ref, source, amp):
    for k in range(ROWS):
        for j in range(COLS):
            source[pl.ds((k * COLS + j) * BINS, BINS), :] = g_ref[j, k].astype(jnp.float32)
    amp[0:HALF] = low_ref[...].astype(jnp.float32)
    amp[BINS + HALF:BINS + 2 * HALF] = high_ref[...].astype(jnp.float32)
    for f in range(BINS):
        real = x_ref[0, f].astype(jnp.float32)
        imag = x_ref[1, f].astype(jnp.float32)
        amp[HALF + f] = jnp.sqrt(real * real + imag * imag).astype(jnp.bfloat16).astype(jnp.float32)
    lane = lax.broadcasted_iota(jnp.int32, (ROWS * COLS, 2 * WIN), 1)
    for f in range(BINS):
        total = amp[f]
        for offset in range(1, 2 * HALF + 1):
            total = total + amp[f + offset]
        smooth = total / (2 * HALF + 1)
        scale = 1.0 / (smooth + 0.1)
        white = jnp.concatenate(
            [(x_ref[q, f].astype(jnp.float32) * scale).astype(jnp.bfloat16) for q in range(2)], axis=0)
        picked = source[pl.ds(f, ROWS * COLS, stride=BINS), :]
        turned = pltpu.roll(picked, WIN, 1)
        turned = jnp.where(lane < WIN, -turned, turned)
        left = jnp.concatenate([picked.astype(jnp.bfloat16), turned.astype(jnp.bfloat16)], axis=0)
        product = jnp.dot(left, white, preferred_element_type=jnp.float32) * (1.0 / WIN)
        out_ref[0, f] = product[0:WIN].astype(jnp.bfloat16)
        out_ref[1, f] = product[WIN:2 * WIN].astype(jnp.bfloat16)


def edge_amplitude(part):
    values = part.astype(jnp.float32)
    return jnp.sqrt(values[0] * values[0] + values[1] * values[1]).astype(jnp.bfloat16)


def local(spectra, source_index):
    forward = [(i, i + 1) for i in range(BANDS - 1)]
    backward = [(t, s) for s, t in forward]
    low = lax.ppermute(edge_amplitude(spectra[:, BINS - HALF:]), "band", forward)
    high = lax.ppermute(edge_amplitude(spectra[:, :HALF]), "band", backward)
    vmem = pl.BlockSpec(memory_space=pltpu.VMEM)
    rows = pl.pallas_call(
        gather_kernel,
        out_shape=jax.ShapeDtypeStruct((COLS, ROWS, BINS, 2 * WIN), jnp.bfloat16),
        in_specs=[pl.BlockSpec(memory_space=pltpu.SMEM), vmem],
        out_specs=vmem,
        scratch_shapes=[
            pltpu.VMEM((ROWS, BINS, 2 * WIN), jnp.bfloat16),
            pltpu.VMEM((2, HALF, 2 * WIN), jnp.float32),
            pltpu.VMEM((2, ROWS, HALF, 2 * WIN), jnp.float32),
            pltpu.SemaphoreType.DMA((ROWS,)),
            pltpu.SemaphoreType.DMA((ROWS,)),
            pltpu.SemaphoreType.DMA((2, ROWS)),
            pltpu.SemaphoreType.DMA((2, ROWS)),
            pltpu.SemaphoreType.DMA((COLS,)),
            pltpu.SemaphoreType.DMA((COLS,)),
        ],
        compiler_params=pltpu.CompilerParams(collective_id=0, has_side_effects=True),
        cost_estimate=pl.CostEstimate(flops=40_000_000, bytes_accessed=40_000_000, transcendentals=0),
        name="source_rows",
    )(source_index, spectra)
    return pl.pallas_call(
        stack_kernel,
        out_shape=jax.ShapeDtypeStruct((2, BINS, ROWS * COLS, CH), jnp.bfloat16),
        in_specs=[vmem] * 4,
        out_specs=vmem,
        scratch_shapes=[
            pltpu.VMEM((ROWS * COLS * BINS, 2 * WIN), jnp.float32),
            pltpu.VMEM((BINS + 2 * HALF, WIN, CH), jnp.float32),
        ],
        name="stack",
    )(spectra, low, high, rows)


def solution(mesh):
    return jax.shard_map(
        local,
        mesh=mesh,
        in_specs=(P(None, "band", None, "rx"), P()),
        out_specs=P(None, "band", None, "rx"),
        check_vma=False,
    )
```

```python
import functools

import jax
import jax.numpy as jnp
from jax import lax
from jax.experimental import pallas as pl
from jax.experimental.pallas import tpu as pltpu
from jax.sharding import PartitionSpec as P

HALF = 4
BINS = 32
WIN = 64
CH = 128
ROWS = 8
COLS = 8
BANDS = 8
MESH = pl.DeviceIdType.MESH


def rounded_amplitude(real, imag):
    return jnp.sqrt(real * real + imag * imag).astype(jnp.bfloat16)


def whiten_four(x, amp, white, first):
    a = [amp[first + k] for k in range(4 + 2 * HALF)]
    common = ((a[3] + a[4]) + (a[5] + a[6])) + (a[7] + a[8])
    early = a[1] + a[2]
    late = a[9] + a[10]
    sides = (a[0] + early, early + a[9], a[2] + late, late + a[11])
    for k in range(4):
        smooth = (common + sides[k]) / (2 * HALF + 1)
        scale = 1.0 / (smooth + 0.1)
        for q in range(2):
            white[first + k, q * WIN:(q + 1) * WIN] = (
                x[q, first + k].astype(jnp.float32) * scale).astype(jnp.bfloat16)


def coefficients(source, f):
    lane = lax.broadcasted_iota(jnp.int32, (ROWS * COLS, 2 * WIN), 1)
    picked = source[pl.ds(f, ROWS * COLS, stride=BINS), :]
    turned = pltpu.roll(picked, WIN, 1)
    turned = jnp.where(lane < WIN, -turned, turned)
    return jnp.concatenate([picked.astype(jnp.bfloat16), turned.astype(jnp.bfloat16)], axis=0)


def multiply(left, white, out, f):
    product = jnp.dot(left, white[f], preferred_element_type=jnp.float32) * (1.0 / WIN)
    out[0, f] = product[0:WIN].astype(jnp.bfloat16)
    out[1, f] = product[WIN:2 * WIN].astype(jnp.bfloat16)


def correlate_kernel(src_ref, x_hbm, out_ref, x, amp, white, source, left, halo_out, halo_in,
                     rows, edge_out, edge_in, blocks, xs, zs, zr, es, er, js, jr, hs, hr):
    rx = lax.axis_index("rx")
    band = lax.axis_index("band")
    z = lax.div(rx, COLS)
    j = lax.rem(rx, COLS)
    above = lax.rem(band + 1, BANDS)
    below = lax.rem(band + BANDS - 1, BANDS)

    def along_z(d):
        return lax.rem(z + d, ROWS)

    def along_j(d):
        return lax.rem(j + d, COLS)

    barrier = pltpu.get_barrier_semaphore()
    for d in range(ROWS):
        for other in (above, below):
            pl.semaphore_signal(barrier, inc=1, device_id=(along_z(d) * COLS + j, other), device_id_type=MESH)
    for d in range(1, ROWS):
        pl.semaphore_signal(barrier, inc=1, device_id=(along_z(d) * COLS + j, band), device_id_type=MESH)
    for d in range(1, COLS):
        pl.semaphore_signal(barrier, inc=1, device_id=(z * COLS + along_j(d), band), device_id_type=MESH)

    load = pltpu.make_async_copy(x_hbm, x, xs)
    load.start()
    load.wait()

    for k in range(HALF):
        for side, f in ((0, k), (1, BINS - HALF + k)):
            value = rounded_amplitude(x[0, f].astype(jnp.float32), x[1, f].astype(jnp.float32))
            halo_out[side, k] = value
            amp[HALF + f] = value.astype(jnp.float32)

    column = src_ref[rx] - rx * CH
    lane = lax.broadcasted_iota(jnp.int32, (BINS, CH), 1)
    bin_row = lax.broadcasted_iota(jnp.int32, (BINS, CH), 0)
    pick = jnp.where(lane == column, 1.0, 0.0).astype(jnp.float32)
    row = jnp.zeros((BINS, CH), jnp.float32)
    for f in range(BINS):
        one = jnp.where(bin_row == f, pick, 0.0).astype(jnp.bfloat16)
        both = x[:, f].reshape(2 * WIN, CH)
        row = row + lax.dot_general(one, both, (((1,), (1,)), ((), ())),
                                    preferred_element_type=jnp.float32)

    def amplitude(values):
        square = values * values
        return jnp.sqrt(square + pltpu.roll(square, WIN, 1)).astype(jnp.bfloat16).astype(jnp.float32)

    own_amp = amplitude(row)
    edge_out[0] = own_amp[0:HALF]
    edge_out[1] = own_amp[BINS - HALF:BINS]
    rows[z] = row.astype(jnp.bfloat16)

    def amplitude_step(i, carry):
        for k in range(4):
            f = HALF + i * 4 + k
            amp[HALF + f] = rounded_amplitude(
                x[0, f].astype(jnp.float32), x[1, f].astype(jnp.float32)).astype(jnp.float32)
        return carry

    lax.fori_loop(0, (BINS - 2 * HALF) // 4, amplitude_step, 0)

    pl.semaphore_wait(barrier, (ROWS - 1) + (COLS - 1) + 2 * ROWS)

    def edge_copy(side, d, slot):
        other = below if side == 0 else above
        return pltpu.make_async_remote_copy(
            src_ref=edge_out.at[side], dst_ref=edge_in.at[1 - side, slot],
            send_sem=es.at[side, d], recv_sem=er.at[side, d],
            device_id=(along_z(d) * COLS + j, other), device_id_type=MESH)

    def row_copy(d, slot):
        return pltpu.make_async_remote_copy(
            src_ref=rows.at[z], dst_ref=rows.at[slot],
            send_sem=zs.at[d], recv_sem=zr.at[d],
            device_id=(along_z(d) * COLS + j, band), device_id_type=MESH)

    def halo_copy(side):
        other = below if side == 0 else above
        return pltpu.make_async_remote_copy(
            src_ref=halo_out.at[side], dst_ref=halo_in.at[1 - side],
            send_sem=hs.at[side], recv_sem=hr.at[side],
            device_id=(rx, other), device_id_type=MESH)

    for d in range(ROWS):
        for side in range(2):
            edge_copy(side, d, z).start()
    for d in (7, 6, 5, 4, 3, 2, 1):
        row_copy(d, z).start()

    @pl.when(band > 0)
    def _():
        halo_copy(0).start()

    @pl.when(band < BANDS - 1)
    def _():
        halo_copy(1).start()

    def whiten_step(i, carry):
        whiten_four(x, amp, white, HALF + i * 4)
        return carry

    lax.fori_loop(0, (BINS - 2 * HALF) // 4, whiten_step, 0)

    for d in range(1, ROWS):
        row_copy(d, lax.rem(z - d + ROWS, ROWS)).wait_recv()
    for d in range(ROWS):
        for side in range(2):
            edge_copy(side, d, lax.rem(z - d + ROWS, ROWS)).wait_recv()

    has_low = (band > 0).astype(jnp.float32)
    has_high = (band < BANDS - 1).astype(jnp.float32)
    for k in range(ROWS):
        values = rows[k].astype(jnp.float32)
        padded = jnp.concatenate(
            [edge_in[0, k] * has_low, amplitude(values), edge_in[1, k] * has_high], axis=0)
        total = padded[0:BINS]
        for offset in range(1, 2 * HALF + 1):
            total = total + padded[offset:offset + BINS]
        smooth = total / (2 * HALF + 1)
        blocks[j, k] = (values / (smooth + 0.1)).astype(jnp.bfloat16)

    def block_copy(d, slot):
        return pltpu.make_async_remote_copy(
            src_ref=blocks.at[j], dst_ref=blocks.at[slot],
            send_sem=js.at[d], recv_sem=jr.at[d],
            device_id=(z * COLS + along_j(d), band), device_id_type=MESH)

    for d in (4, 3, 5, 2, 6, 1, 7):
        block_copy(d, j).start()
    for d in range(1, ROWS):
        row_copy(d, z).wait_send()
    for d in range(ROWS):
        for side in range(2):
            edge_copy(side, d, z).wait_send()
    for d in range(1, COLS):
        block_copy(d, lax.rem(j - d + COLS, COLS)).wait_recv()

    for k in range(ROWS):
        for c in range(COLS):
            source[pl.ds((k * COLS + c) * BINS, BINS), :] = blocks[c, k].astype(jnp.float32)

    def multiply_step(i, carry):
        for k in range(4):
            f = HALF + i * 4 + k
            multiply(coefficients(source, f), white, out_ref, f)
        return carry

    lax.fori_loop(0, (BINS - 2 * HALF) // 4, multiply_step, 0)
    for k in range(HALF):
        left[k] = coefficients(source, k)
        left[HALF + k] = coefficients(source, BINS - HALF + k)

    @pl.when(band == 0)
    def _():
        halo_in[0] = jnp.zeros_like(halo_in[0])

    @pl.when(band > 0)
    def _():
        halo_copy(1).wait_recv()

    for k in range(HALF):
        amp[k] = halo_in[0, k].astype(jnp.float32)
    whiten_four(x, amp, white, 0)
    for k in range(HALF):
        multiply(left[k], white, out_ref, k)

    @pl.when(band == BANDS - 1)
    def _():
        halo_in[1] = jnp.zeros_like(halo_in[1])

    @pl.when(band < BANDS - 1)
    def _():
        halo_copy(0).wait_recv()

    for k in range(HALF):
        amp[BINS + HALF + k] = halo_in[1, k].astype(jnp.float32)
    whiten_four(x, amp, white, BINS - HALF)
    for k in range(HALF):
        multiply(left[HALF + k], white, out_ref, BINS - HALF + k)

    @pl.when(band > 0)
    def _():
        halo_copy(0).wait_send()

    @pl.when(band < BANDS - 1)
    def _():
        halo_copy(1).wait_send()

    for d in range(1, COLS):
        block_copy(d, j).wait_send()


def local(spectra, source_index):
    return pl.pallas_call(
        correlate_kernel,
        out_shape=jax.ShapeDtypeStruct((2, BINS, ROWS * COLS, CH), jnp.bfloat16),
        in_specs=[pl.BlockSpec(memory_space=pltpu.SMEM), pl.BlockSpec(memory_space=pl.ANY)],
        out_specs=pl.BlockSpec(memory_space=pltpu.VMEM),
        scratch_shapes=[
            pltpu.VMEM((2, BINS, WIN, CH), jnp.bfloat16),
            pltpu.VMEM((BINS + 2 * HALF, WIN, CH), jnp.float32),
            pltpu.VMEM((BINS, 2 * WIN, CH), jnp.bfloat16),
            pltpu.VMEM((ROWS * COLS * BINS, 2 * WIN), jnp.float32),
            pltpu.VMEM((2 * HALF, 2 * WIN, 2 * WIN), jnp.bfloat16),
            pltpu.VMEM((2, HALF, WIN, CH), jnp.bfloat16),
            pltpu.VMEM((2, HALF, WIN, CH), jnp.bfloat16),
            pltpu.VMEM((ROWS, BINS, 2 * WIN), jnp.bfloat16),
            pltpu.VMEM((2, HALF, 2 * WIN), jnp.float32),
            pltpu.VMEM((2, ROWS, HALF, 2 * WIN), jnp.float32),
            pltpu.VMEM((COLS, ROWS, BINS, 2 * WIN), jnp.bfloat16),
            pltpu.SemaphoreType.DMA,
            pltpu.SemaphoreType.DMA((ROWS,)),
            pltpu.SemaphoreType.DMA((ROWS,)),
            pltpu.SemaphoreType.DMA((2, ROWS)),
            pltpu.SemaphoreType.DMA((2, ROWS)),
            pltpu.SemaphoreType.DMA((COLS,)),
            pltpu.SemaphoreType.DMA((COLS,)),
            pltpu.SemaphoreType.DMA((2,)),
            pltpu.SemaphoreType.DMA((2,)),
        ],
        compiler_params=pltpu.CompilerParams(collective_id=0, has_side_effects=True),
        name="correlate",
    )(source_index, spectra)


def solution(mesh):
    return jax.shard_map(
        local,
        mesh=mesh,
        in_specs=(P(None, "band", None, "rx"), P()),
        out_specs=P(None, "band", None, "rx"),
        check_vma=False,
    )
```

```python
import functools

import jax
import jax.numpy as jnp
from jax import lax
from jax.experimental import pallas as pl
from jax.experimental.pallas import tpu as pltpu
from jax.sharding import PartitionSpec as P

HALF = 4
BINS = 32
WIN = 64
CH = 128
ROWS = 8
COLS = 8
BANDS = 8
PART = 4
MESH = pl.DeviceIdType.MESH


def rounded_amplitude(real, imag):
    return jnp.sqrt(real * real + imag * imag).astype(jnp.bfloat16)


def whiten_four(x, amp, white, first):
    a = [amp[first + k] for k in range(4 + 2 * HALF)]
    common = ((a[3] + a[4]) + (a[5] + a[6])) + (a[7] + a[8])
    early = a[1] + a[2]
    late = a[9] + a[10]
    sides = (a[0] + early, early + a[9], a[2] + late, late + a[11])
    for k in range(4):
        smooth = (common + sides[k]) / (2 * HALF + 1)
        scale = 1.0 / (smooth + 0.1)
        for q in range(2):
            white[first + k, q * WIN:(q + 1) * WIN] = (
                x[q, first + k].astype(jnp.float32) * scale).astype(jnp.bfloat16)


def coefficients(source, f):
    lane = lax.broadcasted_iota(jnp.int32, (ROWS * COLS, 2 * WIN), 1)
    picked = source[pl.ds(f, ROWS * COLS, stride=BINS), :]
    turned = pltpu.roll(picked, WIN, 1)
    turned = jnp.where(lane < WIN, -turned, turned)
    return jnp.concatenate([picked.astype(jnp.bfloat16), turned.astype(jnp.bfloat16)], axis=0)


def multiply(left, white, out, f):
    product = jnp.dot(left, white[f], preferred_element_type=jnp.float32) * (1.0 / WIN)
    out[0, f] = product[0:WIN].astype(jnp.bfloat16)
    out[1, f] = product[WIN:2 * WIN].astype(jnp.bfloat16)


def correlate_kernel(src_ref, x_hbm, out_ref, x, amp, white, source, left, halo_out, halo_in,
                     rows, edge_out, edge_in, blocks, xs, zs, zr, es, er, js, jr, ts, tr, hs, hr):
    rx = lax.axis_index("rx")
    band = lax.axis_index("band")
    z = lax.div(rx, COLS)
    j = lax.rem(rx, COLS)
    above = lax.rem(band + 1, BANDS)
    below = lax.rem(band + BANDS - 1, BANDS)

    def along_z(d):
        return lax.rem(z + d, ROWS)

    core = lax.rem(j, 2)
    partner = j + 1 - 2 * core

    def along_x(d):
        return lax.rem(j + 2 * d, COLS)

    barrier = pltpu.get_barrier_semaphore()
    for d in range(ROWS):
        for other in (above, below):
            pl.semaphore_signal(barrier, inc=1, device_id=(along_z(d) * COLS + j, other), device_id_type=MESH)
    for d in range(1, ROWS):
        pl.semaphore_signal(barrier, inc=1, device_id=(along_z(d) * COLS + j, band), device_id_type=MESH)
    for d in range(1, COLS // 2):
        pl.semaphore_signal(barrier, inc=1, device_id=(z * COLS + along_x(d), band), device_id_type=MESH)
    pl.semaphore_signal(barrier, inc=1, device_id=(z * COLS + partner, band), device_id_type=MESH)

    load = pltpu.make_async_copy(x_hbm, x, xs)
    load.start()
    load.wait()

    for k in range(HALF):
        for side, f in ((0, k), (1, BINS - HALF + k)):
            value = rounded_amplitude(x[0, f].astype(jnp.float32), x[1, f].astype(jnp.float32))
            halo_out[side, k] = value
            amp[HALF + f] = value.astype(jnp.float32)

    column = src_ref[rx] - rx * CH
    lane = lax.broadcasted_iota(jnp.int32, (BINS, CH), 1)
    bin_row = lax.broadcasted_iota(jnp.int32, (BINS, CH), 0)
    pick = jnp.where(lane == column, 1.0, 0.0).astype(jnp.float32)
    row = jnp.zeros((BINS, CH), jnp.float32)
    for f in range(BINS):
        one = jnp.where(bin_row == f, pick, 0.0).astype(jnp.bfloat16)
        both = x[:, f].reshape(2 * WIN, CH)
        row = row + lax.dot_general(one, both, (((1,), (1,)), ((), ())),
                                    preferred_element_type=jnp.float32)

    def amplitude(values):
        square = values * values
        return jnp.sqrt(square + pltpu.roll(square, WIN, 1)).astype(jnp.bfloat16).astype(jnp.float32)

    own_amp = amplitude(row)
    edge_out[0] = own_amp[0:HALF].astype(jnp.bfloat16)
    edge_out[1] = own_amp[BINS - HALF:BINS].astype(jnp.bfloat16)
    rows[z] = row.astype(jnp.bfloat16)

    pl.semaphore_wait(barrier, (ROWS - 1) + COLS // 2 + 2 * ROWS)

    def edge_copy(side, d, slot):
        other = below if side == 0 else above
        return pltpu.make_async_remote_copy(
            src_ref=edge_out.at[side], dst_ref=edge_in.at[1 - side, slot],
            send_sem=es.at[side, d], recv_sem=er.at[side, d],
            device_id=(along_z(d) * COLS + j, other), device_id_type=MESH)

    def row_copy(d, slot):
        return pltpu.make_async_remote_copy(
            src_ref=rows.at[z], dst_ref=rows.at[slot],
            send_sem=zs.at[d], recv_sem=zr.at[d],
            device_id=(along_z(d) * COLS + j, band), device_id_type=MESH)

    even = lax.rem(band, 2) == 0
    odd = lax.rem(band, 2) == 1

    def halo_copy(side):
        other = below if side == 0 else above
        return pltpu.make_async_remote_copy(
            src_ref=halo_out.at[side], dst_ref=halo_in.at[1 - side],
            send_sem=hs.at[side], recv_sem=hr.at[side],
            device_id=(rx, other), device_id_type=MESH)

    for d in range(ROWS):
        for side in range(2):
            edge_copy(side, d, z).start()
    for d in (7, 6, 5, 4, 3, 2, 1):
        row_copy(d, z).start()


    def start_halo(group):
        @pl.when(jnp.logical_and(group, band > 0))
        def _():
            halo_copy(0).start()

        @pl.when(jnp.logical_and(group, band < BANDS - 1))
        def _():
            halo_copy(1).start()

    def amplitude_step(i, carry):
        for k in range(4):
            f = HALF + i * 4 + k
            amp[HALF + f] = rounded_amplitude(
                x[0, f].astype(jnp.float32), x[1, f].astype(jnp.float32)).astype(jnp.float32)
        return carry

    lax.fori_loop(0, (BINS - 2 * HALF) // 4, amplitude_step, 0)

    def whiten_step(i, carry):
        whiten_four(x, amp, white, HALF + i * 4)
        return carry

    lax.fori_loop(0, (BINS - 2 * HALF) // 4, whiten_step, 0)

    start_halo(odd)


    for d in range(1, ROWS):
        row_copy(d, lax.rem(z - d + ROWS, ROWS)).wait_recv()
    for d in range(ROWS):
        for side in range(2):
            edge_copy(side, d, lax.rem(z - d + ROWS, ROWS)).wait_recv()

    has_low = (band > 0).astype(jnp.float32)
    has_high = (band < BANDS - 1).astype(jnp.float32)
    def block_copy(d, slot, h):
        part = pl.ds(h * PART, PART)
        return pltpu.make_async_remote_copy(
            src_ref=blocks.at[j, part], dst_ref=blocks.at[slot, part],
            send_sem=js.at[d, h], recv_sem=jr.at[d, h],
            device_id=(z * COLS + along_x(d), band), device_id_type=MESH)

    def twin_copy(d, slot, h):
        part = pl.ds(h * PART, PART)
        return pltpu.make_async_remote_copy(
            src_ref=blocks.at[slot, part], dst_ref=blocks.at[slot, part],
            send_sem=ts.at[d, h], recv_sem=tr.at[d, h],
            device_id=(z * COLS + partner, band), device_id_type=MESH)

    for h in range(ROWS // PART):
        for k in range(h * PART, (h + 1) * PART):
            values = rows[k].astype(jnp.float32)
            padded = jnp.concatenate(
                [edge_in[0, k].astype(jnp.float32) * has_low, amplitude(values),
                 edge_in[1, k].astype(jnp.float32) * has_high], axis=0)
            total = padded[0:BINS]
            for offset in range(1, 2 * HALF + 1):
                total = total + padded[offset:offset + BINS]
            smooth = total / (2 * HALF + 1)
            blocks[j, k] = (values / (smooth + 0.1)).astype(jnp.bfloat16)
        for d in (2, 1, 3):
            block_copy(d, j, h).start()
        twin_copy(0, j, h).start()
    for h in range(ROWS // PART):
        for d in (1, 3, 2):
            slot = lax.rem(j - 2 * d + COLS, COLS)
            block_copy(d, slot, h).wait_recv()
            twin_copy(d, slot, h).start()

    start_halo(even)

    for d in range(1, ROWS):
        row_copy(d, z).wait_send()
    for d in range(ROWS):
        for side in range(2):
            edge_copy(side, d, z).wait_send()
    for h in range(ROWS // PART):
        for d in (0, 1, 3, 2):
            twin_copy(d, lax.rem(partner - 2 * d + COLS, COLS), h).wait_recv()

    for k in range(ROWS):
        for c in range(COLS):
            source[pl.ds((k * COLS + c) * BINS, BINS), :] = blocks[c, k].astype(jnp.float32)

    for f in range(HALF, BINS - HALF):
        multiply(coefficients(source, f), white, out_ref, f)
    for k in range(HALF):
        left[k] = coefficients(source, k)
        left[HALF + k] = coefficients(source, BINS - HALF + k)

    @pl.when(band == 0)
    def _():
        halo_in[0] = jnp.zeros_like(halo_in[0])

    @pl.when(band > 0)
    def _():
        halo_copy(1).wait_recv()

    for k in range(HALF):
        amp[k] = halo_in[0, k].astype(jnp.float32)
    whiten_four(x, amp, white, 0)
    for k in range(HALF):
        multiply(left[k], white, out_ref, k)

    @pl.when(band == BANDS - 1)
    def _():
        halo_in[1] = jnp.zeros_like(halo_in[1])

    @pl.when(band < BANDS - 1)
    def _():
        halo_copy(0).wait_recv()

    for k in range(HALF):
        amp[BINS + HALF + k] = halo_in[1, k].astype(jnp.float32)
    whiten_four(x, amp, white, BINS - HALF)
    for k in range(HALF):
        multiply(left[HALF + k], white, out_ref, BINS - HALF + k)

    @pl.when(band > 0)
    def _():
        halo_copy(0).wait_send()

    @pl.when(band < BANDS - 1)
    def _():
        halo_copy(1).wait_send()

    for h in range(ROWS // PART):
        for d in range(1, COLS // 2):
            block_copy(d, j, h).wait_send()
        for d in range(COLS // 2):
            twin_copy(d, lax.rem(j - 2 * d + COLS, COLS), h).wait_send()


def local(spectra, source_index):
    return pl.pallas_call(
        correlate_kernel,
        out_shape=pltpu.VMEM((2, BINS, ROWS * COLS, CH), jnp.bfloat16),
        in_specs=[pl.BlockSpec(memory_space=pltpu.SMEM), pl.BlockSpec(memory_space=pl.ANY)],
        out_specs=pl.BlockSpec(memory_space=pltpu.VMEM),
        scratch_shapes=[
            pltpu.VMEM((2, BINS, WIN, CH), jnp.bfloat16),
            pltpu.VMEM((BINS + 2 * HALF, WIN, CH), jnp.float32),
            pltpu.VMEM((BINS, 2 * WIN, CH), jnp.bfloat16),
            pltpu.VMEM((ROWS * COLS * BINS, 2 * WIN), jnp.float32),
            pltpu.VMEM((2 * HALF, 2 * WIN, 2 * WIN), jnp.bfloat16),
            pltpu.VMEM((2, HALF, WIN, CH), jnp.bfloat16),
            pltpu.VMEM((2, HALF, WIN, CH), jnp.bfloat16),
            pltpu.VMEM((ROWS, BINS, 2 * WIN), jnp.bfloat16),
            pltpu.VMEM((2, HALF, 2 * WIN), jnp.bfloat16),
            pltpu.VMEM((2, ROWS, HALF, 2 * WIN), jnp.bfloat16),
            pltpu.VMEM((COLS, ROWS, BINS, 2 * WIN), jnp.bfloat16),
            pltpu.SemaphoreType.DMA,
            pltpu.SemaphoreType.DMA((ROWS,)),
            pltpu.SemaphoreType.DMA((ROWS,)),
            pltpu.SemaphoreType.DMA((2, ROWS)),
            pltpu.SemaphoreType.DMA((2, ROWS)),
            pltpu.SemaphoreType.DMA((COLS // 2, ROWS // PART)),
            pltpu.SemaphoreType.DMA((COLS // 2, ROWS // PART)),
            pltpu.SemaphoreType.DMA((COLS // 2, ROWS // PART)),
            pltpu.SemaphoreType.DMA((COLS // 2, ROWS // PART)),
            pltpu.SemaphoreType.DMA((2,)),
            pltpu.SemaphoreType.DMA((2,)),
        ],
        compiler_params=pltpu.CompilerParams(collective_id=0, has_side_effects=True),
        name="correlate",
    )(source_index, spectra)


def solution(mesh):
    return jax.shard_map(
        local,
        mesh=mesh,
        in_specs=(P(None, "band", None, "rx"), P()),
        out_specs=P(None, "band", None, "rx"),
        check_vma=False,
    )
```

```python
import functools

import jax
import jax.numpy as jnp
from jax import lax
from jax.experimental import pallas as pl
from jax.experimental.pallas import tpu as pltpu
from jax.sharding import PartitionSpec as P

HALF = 4
BINS = 32
WIN = 64
CH = 128
ROWS = 8
COLS = 8
BANDS = 8
PART = 4
MESH = pl.DeviceIdType.MESH


def rounded_amplitude(real, imag):
    return jnp.sqrt(real * real + imag * imag).astype(jnp.bfloat16)


def whiten_four(x, amp, white, first):
    a = [amp[first + k] for k in range(4 + 2 * HALF)]
    common = ((a[3] + a[4]) + (a[5] + a[6])) + (a[7] + a[8])
    early = a[1] + a[2]
    late = a[9] + a[10]
    sides = (a[0] + early, early + a[9], a[2] + late, late + a[11])
    for k in range(4):
        smooth = (common + sides[k]) / (2 * HALF + 1)
        scale = 1.0 / (smooth + 0.1)
        for q in range(2):
            white[first + k, q * WIN:(q + 1) * WIN] = (
                x[q, first + k].astype(jnp.float32) * scale).astype(jnp.bfloat16)


def coefficients(source, f):
    lane = lax.broadcasted_iota(jnp.int32, (ROWS * COLS, 2 * WIN), 1)
    picked = source[pl.ds(f, ROWS * COLS, stride=BINS), :]
    turned = pltpu.roll(picked, WIN, 1)
    turned = jnp.where(lane < WIN, -turned, turned)
    return jnp.concatenate([picked.astype(jnp.bfloat16), turned.astype(jnp.bfloat16)], axis=0)


def multiply(left, white, out, f):
    product = jnp.dot(left, white[f], preferred_element_type=jnp.float32) * (1.0 / WIN)
    out[0, f] = product[0:WIN].astype(jnp.bfloat16)
    out[1, f] = product[WIN:2 * WIN].astype(jnp.bfloat16)


def correlate_kernel(src_ref, x_hbm, out_ref, x, amp, white, source, left, halo_out, halo_in,
                     rows, edge_out, edge_in, blocks, xs, zs, zr, es, er, js, jr, ts, tr, hs, hr):
    rx = lax.axis_index("rx")
    band = lax.axis_index("band")
    z = lax.div(rx, COLS)
    j = lax.rem(rx, COLS)
    above = lax.rem(band + 1, BANDS)
    below = lax.rem(band + BANDS - 1, BANDS)

    def along_z(d):
        return lax.rem(z + d, ROWS)

    core = lax.rem(j, 2)
    partner = j + 1 - 2 * core

    def along_x(d):
        return lax.rem(j + 2 * d, COLS)

    barrier = pltpu.get_barrier_semaphore()
    def greet(other):
        for d in range(ROWS):
            pl.semaphore_signal(barrier, inc=1, device_id=(along_z(d) * COLS + j, other), device_id_type=MESH)

    @pl.when(band > 0)
    def _():
        greet(below)

    @pl.when(band < BANDS - 1)
    def _():
        greet(above)

    for d in range(1, ROWS):
        pl.semaphore_signal(barrier, inc=1, device_id=(along_z(d) * COLS + j, band), device_id_type=MESH)
    for d in range(1, COLS // 2):
        pl.semaphore_signal(barrier, inc=1, device_id=(z * COLS + along_x(d), band), device_id_type=MESH)
    pl.semaphore_signal(barrier, inc=1, device_id=(z * COLS + partner, band), device_id_type=MESH)

    load = pltpu.make_async_copy(x_hbm, x, xs)
    load.start()
    load.wait()

    for k in range(HALF):
        for side, f in ((0, k), (1, BINS - HALF + k)):
            value = rounded_amplitude(x[0, f].astype(jnp.float32), x[1, f].astype(jnp.float32))
            halo_out[side, k] = value
            amp[HALF + f] = value.astype(jnp.float32)

    column = src_ref[rx] - rx * CH
    lane = lax.broadcasted_iota(jnp.int32, (BINS, CH), 1)
    bin_row = lax.broadcasted_iota(jnp.int32, (BINS, CH), 0)
    pick = jnp.where(lane == column, 1.0, 0.0).astype(jnp.float32)
    row = jnp.zeros((BINS, CH), jnp.float32)
    for f in range(BINS):
        one = jnp.where(bin_row == f, pick, 0.0).astype(jnp.bfloat16)
        both = x[:, f].reshape(2 * WIN, CH)
        row = row + lax.dot_general(one, both, (((1,), (1,)), ((), ())),
                                    preferred_element_type=jnp.float32)

    def amplitude(values):
        square = values * values
        return jnp.sqrt(square + pltpu.roll(square, WIN, 1)).astype(jnp.bfloat16).astype(jnp.float32)

    own_amp = amplitude(row)
    edge_out[0] = own_amp[0:HALF].astype(jnp.bfloat16)
    edge_out[1] = own_amp[BINS - HALF:BINS].astype(jnp.bfloat16)
    rows[z] = row.astype(jnp.bfloat16)

    beside = jnp.where(band > 0, ROWS, 0) + jnp.where(band < BANDS - 1, ROWS, 0)
    pl.semaphore_wait(barrier, (ROWS - 1) + COLS // 2 + beside)

    def edge_copy(side, d, slot):
        other = below if side == 0 else above
        return pltpu.make_async_remote_copy(
            src_ref=edge_out.at[side], dst_ref=edge_in.at[1 - side, slot],
            send_sem=es.at[side, d], recv_sem=er.at[side, d],
            device_id=(along_z(d) * COLS + j, other), device_id_type=MESH)

    def row_copy(d, slot):
        return pltpu.make_async_remote_copy(
            src_ref=rows.at[z], dst_ref=rows.at[slot],
            send_sem=zs.at[d], recv_sem=zr.at[d],
            device_id=(along_z(d) * COLS + j, band), device_id_type=MESH)

    even = lax.rem(band, 2) == 0
    odd = lax.rem(band, 2) == 1

    def halo_copy(side):
        other = below if side == 0 else above
        return pltpu.make_async_remote_copy(
            src_ref=halo_out.at[side], dst_ref=halo_in.at[1 - side],
            send_sem=hs.at[side], recv_sem=hr.at[side],
            device_id=(rx, other), device_id_type=MESH)

    @pl.when(band > 0)
    def _():
        for d in range(ROWS):
            edge_copy(0, d, z).start()

    @pl.when(band < BANDS - 1)
    def _():
        for d in range(ROWS):
            edge_copy(1, d, z).start()

    for d in (7, 6, 5, 4, 3, 2, 1):
        row_copy(d, z).start()

    def start_halo(group):
        @pl.when(jnp.logical_and(group, band > 0))
        def _():
            halo_copy(0).start()

        @pl.when(jnp.logical_and(group, band < BANDS - 1))
        def _():
            halo_copy(1).start()

    def amplitude_step(i, carry):
        for k in range(4):
            f = HALF + i * 4 + k
            amp[HALF + f] = rounded_amplitude(
                x[0, f].astype(jnp.float32), x[1, f].astype(jnp.float32)).astype(jnp.float32)
        return carry

    lax.fori_loop(0, (BINS - 2 * HALF) // 4, amplitude_step, 0)

    def whiten_step(i, carry):
        whiten_four(x, amp, white, HALF + i * 4)
        return carry

    lax.fori_loop(0, (BINS - 2 * HALF) // 4, whiten_step, 0)

    start_halo(odd)

    for d in range(1, ROWS):
        row_copy(d, lax.rem(z - d + ROWS, ROWS)).wait_recv()

    @pl.when(band > 0)
    def _():
        for d in range(ROWS):
            edge_copy(1, d, lax.rem(z - d + ROWS, ROWS)).wait_recv()

    @pl.when(band == 0)
    def _():
        edge_in[0] = jnp.zeros_like(edge_in[0])

    @pl.when(band < BANDS - 1)
    def _():
        for d in range(ROWS):
            edge_copy(0, d, lax.rem(z - d + ROWS, ROWS)).wait_recv()

    @pl.when(band == BANDS - 1)
    def _():
        edge_in[1] = jnp.zeros_like(edge_in[1])

    start_halo(even)

    def block_copy(d, slot, h):
        part = pl.ds(h * PART, PART)
        return pltpu.make_async_remote_copy(
            src_ref=blocks.at[j, part], dst_ref=blocks.at[slot, part],
            send_sem=js.at[d, h], recv_sem=jr.at[d, h],
            device_id=(z * COLS + along_x(d), band), device_id_type=MESH)

    def twin_copy(d, slot, h):
        part = pl.ds(h * PART, PART)
        return pltpu.make_async_remote_copy(
            src_ref=blocks.at[slot, part], dst_ref=blocks.at[slot, part],
            send_sem=ts.at[d, h], recv_sem=tr.at[d, h],
            device_id=(z * COLS + partner, band), device_id_type=MESH)

    for h in range(ROWS // PART):
        for k in range(h * PART, (h + 1) * PART):
            values = rows[k].astype(jnp.float32)
            padded = jnp.concatenate(
                [edge_in[0, k].astype(jnp.float32), amplitude(values),
                 edge_in[1, k].astype(jnp.float32)], axis=0)
            total = padded[0:BINS]
            for offset in range(1, 2 * HALF + 1):
                total = total + padded[offset:offset + BINS]
            smooth = total / (2 * HALF + 1)
            blocks[j, k] = (values / (smooth + 0.1)).astype(jnp.bfloat16)
        for d in (2, 1, 3):
            block_copy(d, j, h).start()
        twin_copy(0, j, h).start()
    for h in range(ROWS // PART):
        for d in (1, 3, 2):
            slot = lax.rem(j - 2 * d + COLS, COLS)
            block_copy(d, slot, h).wait_recv()
            twin_copy(d, slot, h).start()

    for d in range(1, ROWS):
        row_copy(d, z).wait_send()

    @pl.when(band > 0)
    def _():
        for d in range(ROWS):
            edge_copy(0, d, z).wait_send()

    @pl.when(band < BANDS - 1)
    def _():
        for d in range(ROWS):
            edge_copy(1, d, z).wait_send()

    for h in range(ROWS // PART):
        for d in (0, 1, 3, 2):
            twin_copy(d, lax.rem(partner - 2 * d + COLS, COLS), h).wait_recv()

    for k in range(ROWS):
        for c in range(COLS):
            source[pl.ds((k * COLS + c) * BINS, BINS), :] = blocks[c, k].astype(jnp.float32)

    for f in range(HALF, BINS - HALF):
        multiply(coefficients(source, f), white, out_ref, f)
    for k in range(HALF):
        left[k] = coefficients(source, k)
        left[HALF + k] = coefficients(source, BINS - HALF + k)

    @pl.when(band == 0)
    def _():
        halo_in[0] = jnp.zeros_like(halo_in[0])

    @pl.when(band > 0)
    def _():
        halo_copy(1).wait_recv()

    for k in range(HALF):
        amp[k] = halo_in[0, k].astype(jnp.float32)
    whiten_four(x, amp, white, 0)
    for k in range(HALF):
        multiply(left[k], white, out_ref, k)

    @pl.when(band == BANDS - 1)
    def _():
        halo_in[1] = jnp.zeros_like(halo_in[1])

    @pl.when(band < BANDS - 1)
    def _():
        halo_copy(0).wait_recv()

    for k in range(HALF):
        amp[BINS + HALF + k] = halo_in[1, k].astype(jnp.float32)
    whiten_four(x, amp, white, BINS - HALF)
    for k in range(HALF):
        multiply(left[HALF + k], white, out_ref, BINS - HALF + k)

    @pl.when(band > 0)
    def _():
        halo_copy(0).wait_send()

    @pl.when(band < BANDS - 1)
    def _():
        halo_copy(1).wait_send()

    for h in range(ROWS // PART):
        for d in range(1, COLS // 2):
            block_copy(d, j, h).wait_send()
        for d in range(COLS // 2):
            twin_copy(d, lax.rem(j - 2 * d + COLS, COLS), h).wait_send()


def local(spectra, source_index):
    return pl.pallas_call(
        correlate_kernel,
        out_shape=pltpu.VMEM((2, BINS, ROWS * COLS, CH), jnp.bfloat16),
        in_specs=[pl.BlockSpec(memory_space=pltpu.SMEM), pl.BlockSpec(memory_space=pl.ANY)],
        out_specs=pl.BlockSpec(memory_space=pltpu.VMEM),
        scratch_shapes=[
            pltpu.VMEM((2, BINS, WIN, CH), jnp.bfloat16),
            pltpu.VMEM((BINS + 2 * HALF, WIN, CH), jnp.float32),
            pltpu.VMEM((BINS, 2 * WIN, CH), jnp.bfloat16),
            pltpu.VMEM((ROWS * COLS * BINS, 2 * WIN), jnp.float32),
            pltpu.VMEM((2 * HALF, 2 * WIN, 2 * WIN), jnp.bfloat16),
            pltpu.VMEM((2, HALF, WIN, CH), jnp.bfloat16),
            pltpu.VMEM((2, HALF, WIN, CH), jnp.bfloat16),
            pltpu.VMEM((ROWS, BINS, 2 * WIN), jnp.bfloat16),
            pltpu.VMEM((2, HALF, 2 * WIN), jnp.bfloat16),
            pltpu.VMEM((2, ROWS, HALF, 2 * WIN), jnp.bfloat16),
            pltpu.VMEM((COLS, ROWS, BINS, 2 * WIN), jnp.bfloat16),
            pltpu.SemaphoreType.DMA,
            pltpu.SemaphoreType.DMA((ROWS,)),
            pltpu.SemaphoreType.DMA((ROWS,)),
            pltpu.SemaphoreType.DMA((2, ROWS)),
            pltpu.SemaphoreType.DMA((2, ROWS)),
            pltpu.SemaphoreType.DMA((COLS // 2, ROWS // PART)),
            pltpu.SemaphoreType.DMA((COLS // 2, ROWS // PART)),
            pltpu.SemaphoreType.DMA((COLS // 2, ROWS // PART)),
            pltpu.SemaphoreType.DMA((COLS // 2, ROWS // PART)),
            pltpu.SemaphoreType.DMA((2,)),
            pltpu.SemaphoreType.DMA((2,)),
        ],
        compiler_params=pltpu.CompilerParams(collective_id=0, has_side_effects=True),
        name="correlate",
    )(source_index, spectra)


def solution(mesh):
    return jax.shard_map(
        local,
        mesh=mesh,
        in_specs=(P(None, "band", None, "rx"), P()),
        out_specs=P(None, "band", None, "rx"),
        check_vma=False,
    )
```

```python
import functools

import jax
import jax.numpy as jnp
from jax import lax
from jax.experimental import pallas as pl
from jax.experimental.pallas import tpu as pltpu
from jax.sharding import PartitionSpec as P

HALF = 4
BINS = 32
WIN = 64
CH = 128
ROWS = 8
COLS = 8
BANDS = 8
PART = 4
MESH = pl.DeviceIdType.MESH


def rounded_amplitude(real, imag):
    return jnp.sqrt(real * real + imag * imag).astype(jnp.bfloat16)


def whiten_four(x, amp, white, first):
    a = [amp[first + k] for k in range(4 + 2 * HALF)]
    common = ((a[3] + a[4]) + (a[5] + a[6])) + (a[7] + a[8])
    early = a[1] + a[2]
    late = a[9] + a[10]
    sides = (a[0] + early, early + a[9], a[2] + late, late + a[11])
    for k in range(4):
        smooth = (common + sides[k]) / (2 * HALF + 1)
        scale = 1.0 / (smooth + 0.1)
        for q in range(2):
            white[first + k, q * WIN:(q + 1) * WIN] = (
                x[q, first + k].astype(jnp.float32) * scale).astype(jnp.bfloat16)


def coefficients(source, f):
    lane = lax.broadcasted_iota(jnp.int32, (ROWS * COLS, 2 * WIN), 1)
    picked = source[pl.ds(f, ROWS * COLS, stride=BINS), :]
    turned = pltpu.roll(picked, WIN, 1)
    turned = jnp.where(lane < WIN, -turned, turned)
    return jnp.concatenate([picked.astype(jnp.bfloat16), turned.astype(jnp.bfloat16)], axis=0)


def multiply(left, white, out, f):
    product = jnp.dot(left, white[f], preferred_element_type=jnp.float32) * (1.0 / WIN)
    out[0, f] = product[0:WIN].astype(jnp.bfloat16)
    out[1, f] = product[WIN:2 * WIN].astype(jnp.bfloat16)


def correlate_kernel(src_ref, x_hbm, out_ref, x, amp, white, source, left, halo_out, halo_in,
                     rows, edge_out, edge_in, blocks, xs, zs, zr, es, er, js, jr, ts, tr, hs, hr):
    rx = lax.axis_index("rx")
    band = lax.axis_index("band")
    z = lax.div(rx, COLS)
    j = lax.rem(rx, COLS)
    above = lax.rem(band + 1, BANDS)
    below = lax.rem(band + BANDS - 1, BANDS)

    def along_z(d):
        return lax.rem(z + d, ROWS)

    core = lax.rem(j, 2)
    partner = j + 1 - 2 * core

    def along_x(d):
        return lax.rem(j + 2 * d, COLS)

    barrier = pltpu.get_barrier_semaphore()
    def greet(other):
        for d in range(ROWS):
            pl.semaphore_signal(barrier, inc=1, device_id=(along_z(d) * COLS + j, other), device_id_type=MESH)

    @pl.when(band > 0)
    def _():
        greet(below)

    @pl.when(band < BANDS - 1)
    def _():
        greet(above)

    for d in range(1, ROWS):
        pl.semaphore_signal(barrier, inc=1, device_id=(along_z(d) * COLS + j, band), device_id_type=MESH)
    for d in range(1, COLS // 2):
        pl.semaphore_signal(barrier, inc=1, device_id=(z * COLS + along_x(d), band), device_id_type=MESH)
    pl.semaphore_signal(barrier, inc=1, device_id=(z * COLS + partner, band), device_id_type=MESH)

    load = pltpu.make_async_copy(x_hbm, x, xs)
    load.start()
    load.wait()

    for k in range(HALF):
        for side, f in ((0, k), (1, BINS - HALF + k)):
            value = rounded_amplitude(x[0, f].astype(jnp.float32), x[1, f].astype(jnp.float32))
            halo_out[side, k] = value
            amp[HALF + f] = value.astype(jnp.float32)

    column = src_ref[rx] - rx * CH
    lane = lax.broadcasted_iota(jnp.int32, (BINS, CH), 1)
    bin_row = lax.broadcasted_iota(jnp.int32, (BINS, CH), 0)
    pick = jnp.where(lane == column, 1.0, 0.0).astype(jnp.float32)
    row = jnp.zeros((BINS, CH), jnp.float32)
    for f in range(BINS):
        one = jnp.where(bin_row == f, pick, 0.0).astype(jnp.bfloat16)
        both = x[:, f].reshape(2 * WIN, CH)
        row = row + lax.dot_general(one, both, (((1,), (1,)), ((), ())),
                                    preferred_element_type=jnp.float32)

    def amplitude(values):
        square = values * values
        return jnp.sqrt(square + pltpu.roll(square, WIN, 1)).astype(jnp.bfloat16).astype(jnp.float32)

    own_amp = amplitude(row)
    edge_out[0] = own_amp[0:HALF].astype(jnp.bfloat16)
    edge_out[1] = own_amp[BINS - HALF:BINS].astype(jnp.bfloat16)
    rows[z] = row.astype(jnp.bfloat16)

    beside = jnp.where(band > 0, ROWS, 0) + jnp.where(band < BANDS - 1, ROWS, 0)
    pl.semaphore_wait(barrier, (ROWS - 1) + COLS // 2 + beside)

    def edge_copy(side, d, slot):
        other = below if side == 0 else above
        return pltpu.make_async_remote_copy(
            src_ref=edge_out.at[side], dst_ref=edge_in.at[1 - side, slot],
            send_sem=es.at[side, d], recv_sem=er.at[side, d],
            device_id=(along_z(d) * COLS + j, other), device_id_type=MESH)

    def row_copy(d, slot):
        return pltpu.make_async_remote_copy(
            src_ref=rows.at[z], dst_ref=rows.at[slot],
            send_sem=zs.at[d], recv_sem=zr.at[d],
            device_id=(along_z(d) * COLS + j, band), device_id_type=MESH)

    even = lax.rem(band, 2) == 0
    odd = lax.rem(band, 2) == 1

    def halo_copy(side):
        other = below if side == 0 else above
        return pltpu.make_async_remote_copy(
            src_ref=halo_out.at[side], dst_ref=halo_in.at[1 - side],
            send_sem=hs.at[side], recv_sem=hr.at[side],
            device_id=(rx, other), device_id_type=MESH)

    def start_edges():
        @pl.when(band > 0)
        def _():
            for d in range(ROWS):
                edge_copy(0, d, z).start()

        @pl.when(band < BANDS - 1)
        def _():
            for d in range(ROWS):
                edge_copy(1, d, z).start()

    def start_rows():
        for d in (7, 6, 5, 4, 3, 2, 1):
            row_copy(d, z).start()

    @pl.when(odd)
    def _():
        start_edges()

    @pl.when(even)
    def _():
        start_rows()

    @pl.when(odd)
    def _():
        start_rows()

    @pl.when(even)
    def _():
        start_edges()


    def start_halo(group):
        @pl.when(jnp.logical_and(group, band > 0))
        def _():
            halo_copy(0).start()

        @pl.when(jnp.logical_and(group, band < BANDS - 1))
        def _():
            halo_copy(1).start()

    def amplitude_step(i, carry):
        for k in range(4):
            f = HALF + i * 4 + k
            amp[HALF + f] = rounded_amplitude(
                x[0, f].astype(jnp.float32), x[1, f].astype(jnp.float32)).astype(jnp.float32)
        return carry

    lax.fori_loop(0, (BINS - 2 * HALF) // 4, amplitude_step, 0)

    def whiten_step(i, carry):
        whiten_four(x, amp, white, HALF + i * 4)
        return carry

    lax.fori_loop(0, (BINS - 2 * HALF) // 4, whiten_step, 0)

    start_halo(odd)

    for d in range(1, ROWS):
        row_copy(d, lax.rem(z - d + ROWS, ROWS)).wait_recv()

    @pl.when(band > 0)
    def _():
        for d in range(ROWS):
            edge_copy(1, d, lax.rem(z - d + ROWS, ROWS)).wait_recv()

    @pl.when(band == 0)
    def _():
        edge_in[0] = jnp.zeros_like(edge_in[0])

    @pl.when(band < BANDS - 1)
    def _():
        for d in range(ROWS):
            edge_copy(0, d, lax.rem(z - d + ROWS, ROWS)).wait_recv()

    @pl.when(band == BANDS - 1)
    def _():
        edge_in[1] = jnp.zeros_like(edge_in[1])

    start_halo(even)

    def block_copy(d, slot, h):
        part = pl.ds(h * PART, PART)
        return pltpu.make_async_remote_copy(
            src_ref=blocks.at[j, part], dst_ref=blocks.at[slot, part],
            send_sem=js.at[d, h], recv_sem=jr.at[d, h],
            device_id=(z * COLS + along_x(d), band), device_id_type=MESH)

    def twin_copy(d, slot, h):
        part = pl.ds(h * PART, PART)
        return pltpu.make_async_remote_copy(
            src_ref=blocks.at[slot, part], dst_ref=blocks.at[slot, part],
            send_sem=ts.at[d, h], recv_sem=tr.at[d, h],
            device_id=(z * COLS + partner, band), device_id_type=MESH)

    for h in range(ROWS // PART):
        for k in range(h * PART, (h + 1) * PART):
            values = rows[k].astype(jnp.float32)
            padded = jnp.concatenate(
                [edge_in[0, k].astype(jnp.float32), amplitude(values),
                 edge_in[1, k].astype(jnp.float32)], axis=0)
            total = padded[0:BINS]
            for offset in range(1, 2 * HALF + 1):
                total = total + padded[offset:offset + BINS]
            smooth = total / (2 * HALF + 1)
            blocks[j, k] = (values / (smooth + 0.1)).astype(jnp.bfloat16)
        for d in (2, 1, 3):
            block_copy(d, j, h).start()
        twin_copy(0, j, h).start()
    for h in range(ROWS // PART):
        for d in (1, 3, 2):
            slot = lax.rem(j - 2 * d + COLS, COLS)
            block_copy(d, slot, h).wait_recv()
            twin_copy(d, slot, h).start()

    for d in range(1, ROWS):
        row_copy(d, z).wait_send()

    @pl.when(band > 0)
    def _():
        for d in range(ROWS):
            edge_copy(0, d, z).wait_send()

    @pl.when(band < BANDS - 1)
    def _():
        for d in range(ROWS):
            edge_copy(1, d, z).wait_send()

    def widen(slot, h):
        for k in range(h * PART, (h + 1) * PART):
            at = pl.multiple_of((k * COLS + slot) * BINS, BINS)
            source[pl.ds(at, BINS), :] = blocks[slot, k].astype(jnp.float32)

    for h in range(ROWS // PART):
        for d in range(COLS // 2):
            widen(lax.rem(j - 2 * d + COLS, COLS), h)
    for h in range(ROWS // PART):
        for d in (0, 1, 3, 2):
            slot = lax.rem(partner - 2 * d + COLS, COLS)
            twin_copy(d, slot, h).wait_recv()
            widen(slot, h)


    for f in range(HALF, BINS - HALF):
        multiply(coefficients(source, f), white, out_ref, f)
    for k in range(HALF):
        left[k] = coefficients(source, k)
        left[HALF + k] = coefficients(source, BINS - HALF + k)

    @pl.when(band == 0)
    def _():
        halo_in[0] = jnp.zeros_like(halo_in[0])

    @pl.when(band > 0)
    def _():
        halo_copy(1).wait_recv()

    for k in range(HALF):
        amp[k] = halo_in[0, k].astype(jnp.float32)
    whiten_four(x, amp, white, 0)
    for k in range(HALF):
        multiply(left[k], white, out_ref, k)

    @pl.when(band == BANDS - 1)
    def _():
        halo_in[1] = jnp.zeros_like(halo_in[1])

    @pl.when(band < BANDS - 1)
    def _():
        halo_copy(0).wait_recv()

    for k in range(HALF):
        amp[BINS + HALF + k] = halo_in[1, k].astype(jnp.float32)
    whiten_four(x, amp, white, BINS - HALF)
    for k in range(HALF):
        multiply(left[HALF + k], white, out_ref, BINS - HALF + k)

    @pl.when(band > 0)
    def _():
        halo_copy(0).wait_send()

    @pl.when(band < BANDS - 1)
    def _():
        halo_copy(1).wait_send()

    for h in range(ROWS // PART):
        for d in range(1, COLS // 2):
            block_copy(d, j, h).wait_send()
        for d in range(COLS // 2):
            twin_copy(d, lax.rem(j - 2 * d + COLS, COLS), h).wait_send()


def local(spectra, source_index):
    return pl.pallas_call(
        correlate_kernel,
        out_shape=pltpu.VMEM((2, BINS, ROWS * COLS, CH), jnp.bfloat16),
        in_specs=[pl.BlockSpec(memory_space=pltpu.SMEM), pl.BlockSpec(memory_space=pl.ANY)],
        out_specs=pl.BlockSpec(memory_space=pltpu.VMEM),
        scratch_shapes=[
            pltpu.VMEM((2, BINS, WIN, CH), jnp.bfloat16),
            pltpu.VMEM((BINS + 2 * HALF, WIN, CH), jnp.float32),
            pltpu.VMEM((BINS, 2 * WIN, CH), jnp.bfloat16),
            pltpu.VMEM((ROWS * COLS * BINS, 2 * WIN), jnp.float32),
            pltpu.VMEM((2 * HALF, 2 * WIN, 2 * WIN), jnp.bfloat16),
            pltpu.VMEM((2, HALF, WIN, CH), jnp.bfloat16),
            pltpu.VMEM((2, HALF, WIN, CH), jnp.bfloat16),
            pltpu.VMEM((ROWS, BINS, 2 * WIN), jnp.bfloat16),
            pltpu.VMEM((2, HALF, 2 * WIN), jnp.bfloat16),
            pltpu.VMEM((2, ROWS, HALF, 2 * WIN), jnp.bfloat16),
            pltpu.VMEM((COLS, ROWS, BINS, 2 * WIN), jnp.bfloat16),
            pltpu.SemaphoreType.DMA,
            pltpu.SemaphoreType.DMA((ROWS,)),
            pltpu.SemaphoreType.DMA((ROWS,)),
            pltpu.SemaphoreType.DMA((2, ROWS)),
            pltpu.SemaphoreType.DMA((2, ROWS)),
            pltpu.SemaphoreType.DMA((COLS // 2, ROWS // PART)),
            pltpu.SemaphoreType.DMA((COLS // 2, ROWS // PART)),
            pltpu.SemaphoreType.DMA((COLS // 2, ROWS // PART)),
            pltpu.SemaphoreType.DMA((COLS // 2, ROWS // PART)),
            pltpu.SemaphoreType.DMA((2,)),
            pltpu.SemaphoreType.DMA((2,)),
        ],
        compiler_params=pltpu.CompilerParams(collective_id=0, has_side_effects=True),
        name="correlate",
    )(source_index, spectra)


def solution(mesh):
    return jax.shard_map(
        local,
        mesh=mesh,
        in_specs=(P(None, "band", None, "rx"), P()),
        out_specs=P(None, "band", None, "rx"),
        check_vma=False,
    )
```
